256 devices in a mesh: center: 16 (over z, y_lo), batch: 16 (over x, y_hi, core).
Axes of the slice: x: 4, y: 4 (y_hi: 2, y_lo: 2; y = y_hi * 2 + y_lo), z: 8, core: 2. Of those that a mesh axis runs over, the one named last changes fastest.
Arguments:
- batch_points: float32 [32768, 1024], P(('batch', 'center')), as said below
- targets: float32 [32768, 256], P(('batch', 'center')), may hold values from -6 to 6
- centers: float32 [4096, 1024], P('center'), as said below
- weights: float32 [4096, 256], P('center'), may hold values from -0.09375 to 0.09375
- eigen_basis: float32 [4096, 512], P('center'), may hold values from -0.09375 to 0.09375
- shrink: float32 [512], replicated, may hold values from 0 to 0.9
Outputs:
- residual: float32 [32768, 256], P(('batch', 'center'))
- updated: float32 [4096, 256], P('center')
The draws below stay inside these ranges and needn't reach their ends.
Inputs may be any that keep to these rules, and one draw needn't show every extreme that they name: `batch_points`: minibatch points and centers follow one law. Minibatch points and centers follow one law.
All inputs are finite; a program needn't handle non-finite values.
Results may differ from the reference program's by a relative error of at most 0.0001.
Values sent between devices are 32-bit elements; how exact they have to be, the bound alone decides.
No kernel may reach another device: no remote copies, remote signals or barrier semaphores. Data moves between devices by JAX's collectives and lax.ppermute only.
A program may use at most 64 MiB of HBM per device.

```python
import math
import jax
import jax.numpy as jnp
from jax import lax

FEAT = 1024
TARGETS = 256
RANK = 512
CENTERS = 4096
BATCH = 32768
N_BATCH = 16


cluster_count = 32


latent_dims = 8


centroid_scale = 0.7


latent_scale = 0.35


jitter_scale = 0.5


def shared_frame(base_key):
    splits = jax.random.split(jax.random.fold_in(base_key, 7), 2)
    centroids = jnp.clip(jax.random.normal(splits[0], (cluster_count, FEAT), jnp.float32), -4.0, 4.0)
    loading = jnp.clip(jax.random.normal(splits[1], (latent_dims, FEAT), jnp.float32), -4.0, 4.0)
    return (centroids * (centroid_scale / math.sqrt(FEAT)), loading / math.sqrt(FEAT))


def scaled_points(own_key, base_key, row_count):
    centroids, loading = shared_frame(base_key)
    splits = jax.random.split(own_key, 4)
    labels = jax.random.randint(splits[0], (row_count,), 0, cluster_count)
    chosen = jnp.take(centroids, labels, axis=0)
    latent = jnp.clip(jax.random.normal(splits[1], (row_count, latent_dims), jnp.float32), -4.0, 4.0)
    jitter = jnp.clip(jax.random.normal(splits[2], (row_count, FEAT), jnp.float32), -4.0, 4.0)
    factor = jnp.exp(jax.random.uniform(splits[3], (row_count,), jnp.float32, math.log(0.7), math.log(1.4)))
    spread = latent_scale * jnp.dot(latent, loading, precision=lax.Precision.HIGHEST, preferred_element_type=jnp.float32)
    points = chosen + spread + jitter * (jitter_scale / math.sqrt(FEAT))
    return points * factor[:, None]


def draw_batch_points(key, part):
    return scaled_points(jax.random.fold_in(key, 11), key, BATCH)


def draw_centers(key, part):
    return scaled_points(jax.random.fold_in(key, 23), key, CENTERS)


def shard_levels(stream_key, extent, pieces, least, high):
    level, own = 1.0, jax.random.fold_in(stream_key, 6)
    for axis_at, blocks in pieces:
        draws = jnp.exp(jax.random.uniform(jax.random.fold_in(own, axis_at), (blocks,), jnp.float32, least / len(pieces), high / len(pieces)))
        level = level * jnp.repeat(draws, extent[axis_at] // blocks).reshape([-1 if axis == axis_at else 1 for axis in range(len(extent))])
    return level


def centred(key, shape, scale, limit, cuts=(), kind=jnp.bfloat16):
    array = scale * jax.random.normal(key, shape, jnp.float32)
    if cuts:
        array = array * shard_levels(key, shape, cuts, -0.22, 0.18)
    return jnp.clip(array, -limit, limit).astype(kind)


def setup_inputs(seed: int = 0) -> dict:
    keys = jax.random.split(jax.random.key(seed), 7)
    batch_points = draw_batch_points(jax.random.fold_in(keys[6], 71), 0)
    targets = centred(keys[1], (BATCH, TARGETS), 1.0, 6.0, ((0, 256),), jnp.float32)
    centers = draw_centers(jax.random.fold_in(keys[6], 71), 0)
    weights = centred(keys[3], (CENTERS, TARGETS), CENTERS ** -0.5, 0.09375, ((0, 16),), jnp.float32)
    eigen_basis = centred(keys[4], (CENTERS, RANK), CENTERS ** -0.5, 0.09375, ((0, 16),), jnp.float32)
    shrink = jnp.clip(jax.random.uniform(keys[5], (RANK,), jnp.float32, 0.0, 0.9), 0.0, 0.9)
    return {"batch_points": batch_points, "targets": targets, "centers": centers, "weights": weights, "eigen_basis": eigen_basis, "shrink": shrink}


step_size = 4.0

def kernel_tile(points, centers):
    cross = jnp.dot(points, centers.T, precision=lax.Precision.HIGHEST, preferred_element_type=jnp.float32)
    squared = lax.optimization_barrier(jnp.sum(points * points, axis=1))[:, None] + lax.optimization_barrier(jnp.sum(centers * centers, axis=1))[None, :] - 2.0 * cross
    return jnp.exp(-jnp.sqrt(squared))

def reference(batch_points, targets, centers, weights, eigen_basis, shrink):
    group_rows = BATCH // N_BATCH
    points_blocks = batch_points.reshape(N_BATCH, group_rows, FEAT)
    target_blocks = targets.reshape(N_BATCH, group_rows, TARGETS)

    def one_group(carry, pair):
        points, wanted = pair
        tile = kernel_tile(points, centers)
        prediction = jnp.dot(tile, weights, precision=lax.Precision.HIGHEST, preferred_element_type=jnp.float32)
        resid = prediction - wanted
        part = lax.dot_general(tile, resid, (((0,), (0,)), ((), ())), precision=lax.Precision.HIGHEST, preferred_element_type=jnp.float32)
        return (carry + part, resid)
    start = jnp.zeros((CENTERS, TARGETS), jnp.float32)
    summed, resid_blocks = lax.scan(one_group, start, (points_blocks, target_blocks))
    gradient = summed / jnp.sqrt(jnp.float32(BATCH))
    projected = lax.dot_general(eigen_basis, gradient, (((0,), (0,)), ((), ())), precision=lax.Precision.HIGHEST, preferred_element_type=jnp.float32)
    correction = jnp.dot(eigen_basis, shrink[:, None] * projected, precision=lax.Precision.HIGHEST, preferred_element_type=jnp.float32)
    updated = weights - step_size * (gradient - correction)
    return (resid_blocks.reshape(BATCH, TARGETS), updated)
```

```python
import math

import jax
import jax.numpy as jnp
from jax import lax
from jax.experimental import pallas as pl
from jax.experimental.pallas import tpu as pltpu
from jax.sharding import PartitionSpec as P

step_size = 4.0
HI = lax.Precision.HIGHEST
AXES = ("center", "batch")


def decode(i):
    c, b = divmod(i, 16)
    return dict(zp=c // 4, zl=(c // 2) % 2, yl=c % 2, x=b // 4, yh=(b // 2) % 2, core=b % 2)


def encode(d):
    c = (d["zp"] % 4) * 4 + (d["zl"] % 2) * 2 + d["yl"] % 2
    return c * 16 + (d["x"] % 4) * 4 + (d["yh"] % 2) * 2 + d["core"] % 2


def send(value, **shift):
    pairs = []
    for i in range(256):
        d = decode(i)
        for name, by in shift.items():
            d[name] += by
        pairs.append((i, encode(d)))
    return lax.ppermute(value, AXES, pairs)


def dot_t(a, b):
    return lax.dot_general(
        a, b, (((1,), (1,)), ((), ())), precision=HI, preferred_element_type=jnp.float32
    )


def tile_kernel(at, *refs):
    rows, (own_c, own_w), foreign = refs[:4], refs[4:6], refs[6:14]
    tile, pred, cs, ws = refs[14:]
    x, core = at[0], at[1]
    cs[0:256, :] = own_c[...]
    ws[0:256, :] = own_w[...]
    for k in range(4):
        for swapped in range(2):
            src = foreign[swapped * 4 + k]
            sub = lax.rem(x + k, 4) * 2 + lax.rem(core + swapped, 2)
            for m in range(1, 4):
                to = pl.multiple_of(m * 256 + sub * 32, 32)
                cs[pl.ds(to, 32), :] = src[(m - 1) * 32 : m * 32, 0:1024]
                ws[pl.ds(to, 32), :] = src[(m - 1) * 32 : m * 32, 1024:1280]
    ones = jnp.ones((8, 1024), jnp.float32)
    for m in range(4):
        cols = slice(m * 256, (m + 1) * 256)
        block = cs[cols, :]
        norm_c = dot_t(ones, block * block)[0:1, :]
        for p in range(4):
            points = rows[p][...]
            norm_p = jnp.sum(points * points, axis=1, keepdims=True)
            squared = norm_p + norm_c - 2.0 * dot_t(points, block)
            value = jnp.exp(-jnp.sqrt(squared))
            tile[p * 128 : (p + 1) * 128, cols] = value
            part = jnp.dot(value, ws[cols, :], precision=HI, preferred_element_type=jnp.float32)
            if m == 0:
                pred[p] = part
            else:
                pred[p] += part


def kernel_tile(at, rows, own, foreign):
    vmem = pl.BlockSpec(memory_space=pltpu.VMEM)
    return pl.pallas_call(
        tile_kernel,
        in_specs=[pl.BlockSpec(memory_space=pltpu.SMEM)] + [vmem] * 14,
        out_specs=[vmem, vmem],
        out_shape=[
            jax.ShapeDtypeStruct((512, 1024), jnp.float32),
            jax.ShapeDtypeStruct((4, 128, 256), jnp.float32),
        ],
        scratch_shapes=[
            pltpu.VMEM((1024, 1024), jnp.float32),
            pltpu.VMEM((1024, 256), jnp.float32),
        ],
        compiler_params=pltpu.CompilerParams(vmem_limit_bytes=48 << 20),
    )(at, *rows, *own, *foreign)


BLOCK = ({}, {"zl": 1}, {"yl": 1}, {"zl": 1, "yl": 1})


def part(value, index, size, axis):
    return lax.dynamic_slice_in_dim(value, index * size, size, axis)


def on_device(batch_points, targets, centers, weights, eigen_basis, shrink):
    total_rows = 32768
    c, b = lax.axis_index("center"), lax.axis_index("batch")
    x, core = b // 4, b % 2
    sub = x * 2 + core
    mine = jnp.concatenate([part(centers, sub, 32, 0), part(weights, sub, 32, 0)], axis=1)
    along_z = jnp.concatenate([send(mine, zp=-m) for m in (1, 2, 3)], axis=0)
    swap0 = send(along_z, core=1)
    along_x = [along_z] + [send(along_z, x=-k) for k in (1, 2, 3)]
    swapped = [swap0] + [send(v, core=1) for v in along_x[1:]]
    rows = [batch_points] + [send(batch_points, **s) for s in BLOCK[1:]]
    at = jnp.stack([x, core]).astype(jnp.int32)
    tile, pred = kernel_tile(at, rows, (centers, weights), (*along_x, *swapped))
    residual = pred[0] - targets
    for s, p in zip(BLOCK[1:], (1, 2, 3)):
        residual = residual + send(pred[p], **s)
    group = jnp.concatenate([residual] + [send(residual, **s) for s in BLOCK[1:]], axis=0)
    grad = lax.dot_general(
        group, tile, (((0,), (0,)), ((), ())), precision=HI, preferred_element_type=jnp.float32
    )
    grad = part(grad, core, 128, 0) + send(part(grad, 1 - core, 128, 0), core=1)
    grad = part(grad, x, 32, 0) + sum(
        send(part(grad, (x + k) % 4, 32, 0), x=k) for k in (1, 2, 3)
    )
    grad = grad[:, 0:256] + sum(
        send(grad[:, m * 256 : (m + 1) * 256], zp=m) for m in (1, 2, 3)
    )
    grad = grad * (1.0 / math.sqrt(total_rows))
    projected = jnp.dot(grad, eigen_basis, precision=HI, preferred_element_type=jnp.float32)
    grad = grad + send(grad, yh=1)
    projected = projected + sum(send(projected, **s) for s in BLOCK[1:])
    projected = projected + send(projected, yh=1)
    projected = projected + sum(send(projected, zp=m) for m in (1, 2, 3))
    correction = dot_t(projected * shrink[None, :], eigen_basis)
    change = step_size * (grad - correction)
    gathered = jnp.zeros((4, 32, 256), jnp.float32)
    for k in range(4):
        piece = change if k == 0 else send(change, x=-k)
        gathered = lax.dynamic_update_slice(gathered, piece[None], ((x + k) % 4, 0, 0))
    gathered = gathered.reshape(128, 256)
    other = send(gathered, core=1)
    both = jnp.where(core == 0, jnp.concatenate([gathered, other]), jnp.concatenate([other, gathered]))
    updated = weights - both.T
    return (residual, updated)


def solution(mesh):
    return jax.shard_map(
        on_device,
        mesh=mesh,
        in_specs=(
            P(("batch", "center"), None),
            P(("batch", "center"), None),
            P("center", None),
            P("center", None),
            P("center", None),
            P(),
        ),
        out_specs=(P(("batch", "center"), None), P("center", None)),
        check_vma=False,
    )
```

```python
import functools
import math

import jax
import jax.numpy as jnp
from jax import lax
from jax.experimental import pallas as pl
from jax.experimental.pallas import tpu as pltpu
from jax.sharding import PartitionSpec as P

step_size = 4.0
HI = lax.Precision.HIGHEST
AXES = ("center", "batch")


def decode(i):
    c, b = divmod(i, 16)
    return dict(zp=c // 4, zl=(c // 2) % 2, yl=c % 2, x=b // 4, yh=(b // 2) % 2, core=b % 2)


def encode(d):
    c = (d["zp"] % 4) * 4 + (d["zl"] % 2) * 2 + d["yl"] % 2
    return c * 16 + (d["x"] % 4) * 4 + (d["yh"] % 2) * 2 + d["core"] % 2


def send(value, **shift):
    pairs = []
    for i in range(256):
        d = decode(i)
        for name, by in shift.items():
            d[name] += by
        pairs.append((i, encode(d)))
    return lax.ppermute(value, AXES, pairs)


def dot_t(a, b, precision=None):
    return lax.dot_general(
        a, b, (((1,), (1,)), ((), ())), precision=precision, preferred_element_type=jnp.float32
    )


def halves(value):
    high = value.astype(jnp.bfloat16)
    return high, (value - high.astype(jnp.float32)).astype(jnp.bfloat16)


def three(dot, a, b):
    return dot(a[0], b[0]) + dot(a[0], b[1]) + dot(a[1], b[0])


def dot_first(a, b):
    return lax.dot_general(a, b, (((0,), (0,)), ((), ())), preferred_element_type=jnp.float32)


def rows_kernel(*refs):
    rows, (high, low, norm) = refs[:4], refs[4:]
    ones = jnp.ones((8, 1024), jnp.bfloat16)
    for p in range(4):
        value = rows[p][...]
        to = slice(p * 128, (p + 1) * 128)
        high[to, :], low[to, :] = halves(value)
        first, second = halves(value * value)
        rest = value * value - first.astype(jnp.float32) - second.astype(jnp.float32)
        norm[:, to] = (
            dot_t(ones, first) + dot_t(ones, second) + dot_t(ones, rest.astype(jnp.bfloat16))
        )


def tile_kernel(counts, whole, begin, end, *refs):
    rh, rl, norm = refs[:3]
    n_in = 3 + len(counts) + (1 if whole else 0) + (0 if begin else 1)
    pieces, (th, tl, pred) = refs[3:n_in], refs[n_in : n_in + 3]
    acc = pred if not end else refs[n_in + 3]
    if begin:
        acc[...] = jnp.zeros_like(acc)
    else:
        acc[...] = pieces[-1][...]
    at = 0
    for i, count in enumerate(counts):
        if whole and i == 0:
            center, weight = pieces[0][...], pieces[1][...]
        else:
            ref = pieces[i + whole]
            center, weight = ref[:, 0:1024], ref[:, 1024:1280]
        norm_c = jnp.sum(center * center, axis=1, keepdims=True)
        center, weight = halves(center), halves(weight)
        for r in range(2):
            cols = slice(r * 256, (r + 1) * 256)
            cross = three(dot_t, center, (rh[cols, :], rl[cols, :]))
            squared = norm[0:1, cols] + norm_c - 2.0 * cross
            value = halves(jnp.exp(-jnp.sqrt(squared)))
            th[at : at + count, cols], tl[at : at + count, cols] = value
            acc[:, cols] += three(dot_first, weight, value)
        at += count
    if end:
        for p in range(4):
            pred[p] = acc[:, p * 128 : (p + 1) * 128].T


VMEM = pl.BlockSpec(memory_space=pltpu.VMEM)
SMEM = pl.BlockSpec(memory_space=pltpu.SMEM)
PARAMS = pltpu.CompilerParams(vmem_limit_bytes=40 << 20)


def split_rows(rows):
    return pl.pallas_call(
        rows_kernel,
        in_specs=[VMEM] * 4,
        out_specs=[VMEM] * 3,
        out_shape=[
            jax.ShapeDtypeStruct((512, 1024), jnp.bfloat16),
            jax.ShapeDtypeStruct((512, 1024), jnp.bfloat16),
            jax.ShapeDtypeStruct((8, 512), jnp.float32),
        ],
        compiler_params=PARAMS,
        name="rows",
    )(*rows)


def kernel_tile(rows, own, pieces, acc, end, name):
    counts = ([256] if own else []) + [p.shape[0] for p in pieces]
    total = sum(counts)
    args = [*rows, *(own or ()), *pieces] + ([] if acc is None else [acc])
    pred = (4, 128, 256) if end else (256, 512)
    return pl.pallas_call(
        functools.partial(tile_kernel, counts, bool(own), acc is None, end),
        in_specs=[VMEM] * len(args),
        out_specs=[VMEM] * 3,
        out_shape=[
            jax.ShapeDtypeStruct((total, 512), jnp.bfloat16),
            jax.ShapeDtypeStruct((total, 512), jnp.bfloat16),
            jax.ShapeDtypeStruct(pred, jnp.float32),
        ],
        scratch_shapes=[pltpu.VMEM((256, 512), jnp.float32)] if end else [],
        compiler_params=PARAMS,
        name=name,
    )(*args)


def gradient_kernel(order, at, *refs):
    n = len(order)
    tiles, resid = refs[: 2 * n], refs[2 * n : 2 * n + 4]
    keep, give, th, tl, rh, rl = refs[2 * n + 4 :]
    x, core = at[0], at[1]
    for i in range(n):
        row = 0
        for k, swapped in order[i]:
            if k is None:
                th[0:256, :] = tiles[2 * i][0:256, :]
                tl[0:256, :] = tiles[2 * i + 1][0:256, :]
                row += 256
                continue
            sub = lax.rem(x + k, 4) * 2 + lax.rem(core + swapped, 2)
            for m in range(1, 4):
                to = pl.multiple_of(m * 256 + sub * 32, 32)
                th[pl.ds(to, 32), :] = tiles[2 * i][row : row + 32, :]
                tl[pl.ds(to, 32), :] = tiles[2 * i + 1][row : row + 32, :]
                row += 32
    for p in range(4):
        rh[:, p * 128 : (p + 1) * 128], rl[:, p * 128 : (p + 1) * 128] = halves(resid[p][...].T)
    for out, which in ((give, 1 - core), (keep, core)):
        rows = pl.ds(pl.multiple_of(which * 128, 128), 128)
        left = (rh[rows, :], rl[rows, :])
        for m in range(4):
            cols = slice(m * 256, (m + 1) * 256)
            out[:, cols] = three(dot_t, left, (th[cols, :], tl[cols, :]))


def gradient(order, at, tiles, resid):
    flat = [t for pair in tiles for t in pair]
    return pl.pallas_call(
        functools.partial(gradient_kernel, order),
        in_specs=[SMEM] + [VMEM] * (len(flat) + 4),
        out_specs=[VMEM] * 2,
        out_shape=[jax.ShapeDtypeStruct((128, 1024), jnp.float32)] * 2,
        scratch_shapes=[
            pltpu.VMEM((1024, 512), jnp.bfloat16),
            pltpu.VMEM((1024, 512), jnp.bfloat16),
            pltpu.VMEM((256, 512), jnp.bfloat16),
            pltpu.VMEM((256, 512), jnp.bfloat16),
        ],
        compiler_params=PARAMS,
        name="gradient",
    )(at, *flat, *resid)


BLOCK = ({}, {"zl": 1}, {"yl": 1}, {"zl": 1, "yl": 1})


def part(value, index, size, axis):
    return lax.dynamic_slice_in_dim(value, index * size, size, axis)


def on_device(batch_points, targets, centers, weights, eigen_basis, shrink):
    total_rows = 32768
    c, b = lax.axis_index("center"), lax.axis_index("batch")
    x, core = b // 4, b % 2
    sub = x * 2 + core
    mine = jnp.concatenate([part(centers, sub, 32, 0), part(weights, sub, 32, 0)], axis=1)
    along_z = jnp.concatenate([send(mine, zp=-m) for m in (1, 2, 3)], axis=0)
    swap0 = send(along_z, core=1)
    along_x = [along_z] + [send(along_z, x=-k) for k in (1, 2, 3)]
    swapped = [swap0] + [send(v, core=1) for v in along_x[1:]]
    rows = [batch_points] + [send(batch_points, **s) for s in BLOCK[1:]]
    at = jnp.stack([x, core]).astype(jnp.int32)
    split = split_rows(rows)
    th0, tl0, acc = kernel_tile(
        split, (centers, weights), (along_x[0], swapped[0]), None, False, "tile_a"
    )
    th1, tl1, acc = kernel_tile(
        split, None, (along_x[1], swapped[1], along_x[3], swapped[3]), acc, False, "tile_b"
    )
    th2, tl2, pred = kernel_tile(split, None, (along_x[2], swapped[2]), acc, True, "tile_c")
    residual = pred[0] - targets
    for s, p in zip(BLOCK[1:], (1, 2, 3)):
        residual = residual + send(pred[p], **s)
    group = [residual] + [send(residual, **s) for s in BLOCK[1:]]
    order = (((None, 0), (0, 0), (0, 1)), ((1, 0), (1, 1), (3, 0), (3, 1)), ((2, 0), (2, 1)))
    keep, give = gradient(order, at, ((th0, tl0), (th1, tl1), (th2, tl2)), group)
    grad = keep + send(give, core=1)
    grad = part(grad, x, 32, 0) + sum(
        send(part(grad, (x + k) % 4, 32, 0), x=k) for k in (1, 2, 3)
    )
    grad = grad[:, 0:256] + sum(
        send(grad[:, m * 256 : (m + 1) * 256], zp=m) for m in (1, 2, 3)
    )
    grad = grad * (1.0 / math.sqrt(total_rows))
    projected = jnp.dot(grad, eigen_basis, precision=HI, preferred_element_type=jnp.float32)
    grad = grad + send(grad, yh=1)
    projected = projected + sum(send(projected, **s) for s in BLOCK[1:])
    projected = projected + send(projected, yh=1)
    projected = projected + sum(send(projected, zp=m) for m in (1, 2, 3))
    correction = dot_t(projected * shrink[None, :], eigen_basis, HI)
    change = step_size * (grad - correction)
    gathered = jnp.zeros((4, 32, 256), jnp.float32)
    for k in range(4):
        piece = change if k == 0 else send(change, x=-k)
        gathered = lax.dynamic_update_slice(gathered, piece[None], ((x + k) % 4, 0, 0))
    gathered = gathered.reshape(128, 256)
    other = send(gathered, core=1)
    both = jnp.where(core == 0, jnp.concatenate([gathered, other]), jnp.concatenate([other, gathered]))
    updated = weights - both.T
    return (residual, updated)


def solution(mesh):
    return jax.shard_map(
        on_device,
        mesh=mesh,
        in_specs=(
            P(("batch", "center"), None),
            P(("batch", "center"), None),
            P("center", None),
            P("center", None),
            P("center", None),
            P(),
        ),
        out_specs=(P(("batch", "center"), None), P("center", None)),
        check_vma=False,
    )
```

```python
import functools
import math

import jax
import jax.numpy as jnp
from jax import lax
from jax.experimental import pallas as pl
from jax.experimental.pallas import tpu as pltpu
from jax.sharding import PartitionSpec as P


step_size = 4.0
HI = lax.Precision.HIGHEST
AXES = ("center", "batch")


def decode(i):
    c, b = divmod(i, 16)
    return dict(zp=c // 4, zl=(c // 2) % 2, yl=c % 2, x=b // 4, yh=(b // 2) % 2, core=b % 2)


def encode(d):
    c = (d["zp"] % 4) * 4 + (d["zl"] % 2) * 2 + d["yl"] % 2
    return c * 16 + (d["x"] % 4) * 4 + (d["yh"] % 2) * 2 + d["core"] % 2


def send(value, **shift):
    pairs = []
    for i in range(256):
        d = decode(i)
        for name, by in shift.items():
            d[name] += by
        pairs.append((i, encode(d)))
    return lax.ppermute(value, AXES, pairs)


def dot_t(a, b, precision=None):
    return lax.dot_general(
        a, b, (((1,), (1,)), ((), ())), precision=precision, preferred_element_type=jnp.float32
    )


def halves(value):
    high = value.astype(jnp.bfloat16)
    return high, (value - high.astype(jnp.float32)).astype(jnp.bfloat16)


def exact(value):
    high, low = halves(value)
    rest = value - high.astype(jnp.float32) - low.astype(jnp.float32)
    return high, low, rest.astype(jnp.bfloat16)


def three(dot, a, b):
    return dot(a[0], b[0]) + dot(a[0], b[1]) + dot(a[1], b[0])


def dot_first(a, b):
    return lax.dot_general(a, b, (((0,), (0,)), ((), ())), preferred_element_type=jnp.float32)


def pick_kernel(at, centers, weights, near, far, sems):
    first = pl.multiple_of(at[0] * 64, 64)
    half = pl.multiple_of(at[0] * 64 + at[1] * 32, 32)
    copies = [
        pltpu.make_async_copy(centers.at[pl.ds(first, 64), :], near.at[:, 0:1024], sems.at[0]),
        pltpu.make_async_copy(weights.at[pl.ds(first, 64), :], near.at[:, 1024:1280], sems.at[1]),
        pltpu.make_async_copy(centers.at[pl.ds(half, 32), :], far.at[:, 0:1024], sems.at[2]),
        pltpu.make_async_copy(weights.at[pl.ds(half, 32), :], far.at[:, 1024:1280], sems.at[3]),
    ]
    for copy in copies:
        copy.start()
    for copy in copies:
        copy.wait()


def pick(at, centers, weights):
    return pl.pallas_call(
        pick_kernel,
        in_specs=[SMEM] + [pl.BlockSpec(memory_space=pltpu.HBM)] * 2,
        out_specs=[VMEM] * 2,
        out_shape=[
            jax.ShapeDtypeStruct((64, 1280), jnp.float32),
            jax.ShapeDtypeStruct((32, 1280), jnp.float32),
        ],
        scratch_shapes=[pltpu.SemaphoreType.DMA((4,))],
        compiler_params=params(2),
        name="pick",
    )(at, *(pltpu.with_memory_space_constraint(v, pltpu.HBM) for v in (centers, weights)))


def rows_kernel(*refs):
    rows, (high, low, norm) = refs[:-3], refs[-3:]
    ones = jnp.ones((8, 1024), jnp.bfloat16)
    at = 0
    for ref in rows:
        value = ref[...]
        to = slice(at, at + value.shape[0])
        high[to, :], low[to, :] = halves(value)
        at += value.shape[0]
    for p in range(2):
        to = slice(p * 128, (p + 1) * 128)
        value = high[to, :].astype(jnp.float32) + low[to, :].astype(jnp.float32)
        square = value * value
        norm[:, to] = sum(dot_t(ones, v) for v in exact(square))


def convert_centers(refs, whole, outs):
    ch, cl, wh, wl, norm_c = outs
    at, refs = 0, list(refs)

    def convert(center, weight, at, count):
        to = pl.ds(at, count)
        square = center * center
        lanes = [square[:, i : i + 128] for i in range(0, 1024, 128)]
        norm_c[to, :] = sum(lanes[1:], lanes[0])
        ch[to, :], cl[to, :] = halves(center)
        wh[to, :], wl[to, :] = halves(weight)

    if whole:
        own_c, own_w = refs.pop(0), refs.pop(0)

        def step(i, carry):
            first = pl.multiple_of(i * 64, 64)
            to = pl.ds(first, 64)
            convert(own_c[to, :], own_w[to, :], first, 64)
            return carry

        lax.fori_loop(0, 4, step, 0)
        at = 256
    for ref in refs:
        count = ref.shape[0]
        convert(ref[:, 0:1024], ref[:, 1024:1280], at, count)
        at += count
    ones = jnp.ones((128, 128), jnp.bfloat16)
    norm_c[...] = sum(
        jnp.dot(v, ones, preferred_element_type=jnp.float32) for v in exact(norm_c[...])
    )


def tile_kernel(segments, has_before, *refs):
    refs = list(refs)
    take = lambda n: [refs.pop(0) for _ in range(n)]
    rh, rl, norm = take(3)
    inputs = [take(pieces or 5) for _, pieces, _ in segments]
    before = take(1) if has_before else None
    th, tl, pred = take(3)
    total = before[0][...] if has_before else None
    first = 0
    cross = refs.pop()
    for (count, pieces, whole), given in zip(segments, inputs):
        if pieces:
            centers = take(5)
            convert_centers(given, whole, centers)
        else:
            centers = given
        ch, cl, wh, wl, norm_c = centers
        cross[0:count, :] = three(dot_t, (ch[...], cl[...]), (rh[...], rl[...]))

        def step(i, carry):
            at = pl.multiple_of(i * 128, 128)
            here = pl.ds(at, 128)
            squared = norm[0:1, :] + norm_c[here, 0:1] - 2.0 * cross[here, :]
            to = pl.ds(pl.multiple_of(first + at, 128), 128)
            th[to, :], tl[to, :] = halves(jnp.exp(-jnp.sqrt(squared)))
            return carry

        lax.fori_loop(0, count // 128, step, 0)
        to = slice(first, first + count)
        part = three(dot_first, (wh[...], wl[...]), (th[to, :], tl[to, :]))
        total = part if total is None else total + part
        first += count
    if len(pred.shape) == 3:
        for p in range(2):
            pred[p] = total[:, p * 128 : (p + 1) * 128].T
    else:
        pred[...] = total


VMEM = pl.BlockSpec(memory_space=pltpu.VMEM)
SMEM = pl.BlockSpec(memory_space=pltpu.SMEM)


def params(mib):
    return pltpu.CompilerParams(vmem_limit_bytes=mib << 20)


def split_rows(rows):
    return pl.pallas_call(
        rows_kernel,
        in_specs=[VMEM] * len(rows),
        out_specs=[VMEM] * 3,
        out_shape=[
            jax.ShapeDtypeStruct((256, 1024), jnp.bfloat16),
            jax.ShapeDtypeStruct((256, 1024), jnp.bfloat16),
            jax.ShapeDtypeStruct((8, 256), jnp.float32),
        ],
        compiler_params=params(5),
    )(*rows)


def kernel_tile(side, segments, before, last):
    bf16, f32 = jnp.bfloat16, jnp.float32
    shape = jax.ShapeDtypeStruct
    args, spec, converted, count = list(side), [], [], 0
    for pieces, whole in segments:
        args += pieces
        raw = pieces[0].dtype == f32
        n = sum(p.shape[0] for p in pieces) - (256 if whole else 0) if raw else pieces[0].shape[0]
        spec.append((n, len(pieces) if raw else 0, whole))
        count += n
        if raw:
            converted += [shape((n, 1024), bf16)] * 2 + [shape((n, 256), bf16)] * 2
            converted.append(shape((n, 128), f32))
    args += [] if before is None else [before]
    outs = [shape((count, 256), bf16), shape((count, 256), bf16)]
    outs.append(shape((2, 128, 256) if last else (256, 256), f32))
    outs += converted
    out = pl.pallas_call(
        functools.partial(tile_kernel, spec, before is not None),
        in_specs=[VMEM] * len(args),
        out_specs=[VMEM] * len(outs),
        out_shape=outs,
        scratch_shapes=[pltpu.VMEM((max(n for n, _, _ in spec), 256), f32)],
        compiler_params=params(14),
    )(*args)
    return (out[0], out[1]), out[2], out[3:]


def assemble_kernel(at, *refs):
    tiles, (th, tl) = refs[:10], refs[10:]
    x, core = at[0], at[1]
    for low in range(2):
        full = (th, tl)[low]
        side_a, side_b = tiles[low:6:2], tiles[6 + low :: 2]

        def put(to, count, row):
            for cols, side in ((slice(0, 256), side_a), (slice(256, 512), side_b)):
                at = row
                for tile in side:
                    if 0 <= at < tile.shape[0]:
                        full[to, cols] = tile[at : at + count, :]
                    at -= tile.shape[0]

        put(slice(0, 256), 256, 0)
        for k in range(4):
            for swapped in range(2):
                piece = k * 2 + swapped
                half = lax.rem(core + swapped, 2)
                other = lax.rem(x + k, 4)
                to = pl.multiple_of((1 + 2 * half) * 256 + other * 64, 64)
                put(pl.ds(to, 64), 64, 256 + piece * 64)
                to = pl.multiple_of(512 + other * 64 + half * 32, 32)
                put(pl.ds(to, 32), 32, 768 + piece * 32)


def assemble(at, tiles):
    flat = [t for pair in tiles for t in pair]
    return pl.pallas_call(
        assemble_kernel,
        in_specs=[SMEM] + [VMEM] * len(flat),
        out_specs=[VMEM] * 2,
        out_shape=[jax.ShapeDtypeStruct((1024, 512), jnp.bfloat16)] * 2,
        compiler_params=params(8),
        name="assemble",
    )(at, *flat)


def gradient_kernel(offset, at, *refs):
    th, tl, resid, (out,) = refs[0], refs[1], refs[2:6], refs[6:7]
    rh, rl = refs[7:]
    half = pl.ds(pl.multiple_of(lax.rem(at[1] + offset, 2) * 128, 128), 128)
    for p in range(4):
        cols = slice(p * 128, (p + 1) * 128)
        rh[:, cols], rl[:, cols] = halves(resid[p][:, half].T)
    for m in range(4):
        cols = slice(m * 256, (m + 1) * 256)
        out[:, cols] = three(dot_t, (rh[...], rl[...]), (th[cols, :], tl[cols, :]))


def gradient(at, full, resid, offset):
    return pl.pallas_call(
        functools.partial(gradient_kernel, offset),
        in_specs=[SMEM] + [VMEM] * 6,
        out_specs=VMEM,
        out_shape=jax.ShapeDtypeStruct((128, 1024), jnp.float32),
        scratch_shapes=[pltpu.VMEM((128, 512), jnp.bfloat16)] * 2,
        compiler_params=params(8),
    )(at, *full, *resid)


BLOCK = ({}, {"yl": 1}, {"zl": 1}, {"zl": 1, "yl": 1})


def named(value, **shift):
    return send(value, **shift)


REST = [list(range(core, 16, 2)) for core in range(2)]


def exchange(value):
    return lax.all_to_all(value, "batch", 0, 0, tiled=False, axis_index_groups=REST)


def to_z_neighbours(value):
    pairs = []
    for i in range(256):
        d = decode(i)
        d["zp"] += 1 if d["core"] else -1
        pairs.append((i, encode(d)))
    return lax.ppermute(value, AXES, pairs)


def step(batch_points, targets, centers, weights, eigen_basis, shrink):
    b = lax.axis_index("batch")
    x, core = b // 4, b % 2
    at = jnp.stack([x, core]).astype(jnp.int32)
    near, far = pick(at, centers, weights)
    near = to_z_neighbours(near)
    far = named(far, zp=2)
    rows_y = named(batch_points, yl=1)
    rows_z = named(batch_points, zl=1)
    near = [near] + [named(near, x=-k) for k in (1, 3, 2)]
    rows_d0 = named(rows_y[0:64], zl=1)
    far = [far] + [named(far, x=-k) for k in (1, 3, 2)]
    rows_d1 = named(rows_z[64:128], yl=1)
    near = [near[i] for i in (0, 1, 3, 2)]
    far = [far[i] for i in (0, 1, 3, 2)]
    near = [v for k in range(4) for v in (near[k], named(near[k], core=1))]
    far = [v for k in range(4) for v in (far[k], named(far[k], core=1))]
    side_a = split_rows((batch_points, rows_y))
    side_b = split_rows((rows_z, rows_d0, rows_d1))
    tile_a1, pred_a, first = kernel_tile(
        side_a, [([centers, weights, *near[:2]], True)], None, False
    )
    tile_a2, pred_a, second = kernel_tile(side_a, [(near[2:], False)], pred_a, False)
    tile_b1, pred_b, _ = kernel_tile(side_b, [(first, False), (second, False)], None, False)
    tile_b2, pred_b, third = kernel_tile(side_b, [(far, False)], pred_b, True)
    tile_a3, pred_a, _ = kernel_tile(side_a, [(third, False)], pred_a, True)
    pred = (pred_a[0], pred_a[1], pred_b[0], pred_b[1])
    residual = pred[0] - targets
    for p in (2, 3, 1):
        residual = residual + named(pred[p], **BLOCK[p])
    group = [residual] + [named(residual, **BLOCK[p]) for p in (1, 2, 3)]
    full = assemble(at, (tile_a1, tile_a2, tile_a3, tile_b1, tile_b2))
    give = gradient(at, full, group, 1)
    keep = gradient(at, full, group, 0)
    grad = keep + named(give, core=1)
    grad = jnp.sum(exchange(grad.reshape(8, 16, 1024)), axis=0)
    grad = grad[:, 0:256] + sum(named(grad[:, m * 256 : (m + 1) * 256], zp=m) for m in (2, 1, 3))
    grad = grad * (1.0 / math.sqrt(32768))
    projected = jnp.dot(grad, eigen_basis, precision=HI, preferred_element_type=jnp.float32)
    projected = projected + sum(named(projected, **BLOCK[p]) for p in (3, 1, 2))
    projected = projected + sum(named(projected, zp=m) for m in (2, 1, 3))
    correction = dot_t(projected * shrink[None, :], eigen_basis, HI)
    change = step_size * (grad - correction)
    change = exchange(jnp.broadcast_to(change[None], (8, 16, 256))).reshape(128, 256)
    other = named(change, core=1)
    both = jnp.where(core == 0, jnp.concatenate([change, other]), jnp.concatenate([other, change]))
    updated = weights - both.T
    return (residual, updated)


def solution(mesh):
    return jax.shard_map(
        step,
        mesh=mesh,
        in_specs=(
            P(("batch", "center"), None),
            P(("batch", "center"), None),
            P("center", None),
            P("center", None),
            P("center", None),
            P(),
        ),
        out_specs=(P(("batch", "center"), None), P("center", None)),
        check_vma=False,
    )
```

```python
import functools
import math

import jax
import jax.numpy as jnp
from jax import lax
from jax.experimental import pallas as pl
from jax.experimental.pallas import tpu as pltpu
from jax.sharding import PartitionSpec as P


step_size = 4.0
HI = lax.Precision.HIGHEST
AXES = ("center", "batch")


def decode(i):
    c, b = divmod(i, 16)
    return dict(zp=c // 4, zl=(c // 2) % 2, yl=c % 2, x=b // 4, yh=(b // 2) % 2, core=b % 2)


def encode(d):
    c = (d["zp"] % 4) * 4 + (d["zl"] % 2) * 2 + d["yl"] % 2
    return c * 16 + (d["x"] % 4) * 4 + (d["yh"] % 2) * 2 + d["core"] % 2


def send(value, **shift):
    pairs = []
    for i in range(256):
        d = decode(i)
        for name, by in shift.items():
            d[name] += by
        pairs.append((i, encode(d)))
    return lax.ppermute(value, AXES, pairs)


def dot_t(a, b, precision=None):
    return lax.dot_general(
        a, b, (((1,), (1,)), ((), ())), precision=precision, preferred_element_type=jnp.float32
    )


def halves(value):
    high = value.astype(jnp.bfloat16)
    return high, (value - high.astype(jnp.float32)).astype(jnp.bfloat16)


def exact(value):
    high, low = halves(value)
    rest = value - high.astype(jnp.float32) - low.astype(jnp.float32)
    return high, low, rest.astype(jnp.bfloat16)


def three(dot, a, b):
    return dot(a[0], b[0]) + dot(a[0], b[1]) + dot(a[1], b[0])


def dot_first(a, b):
    return lax.dot_general(a, b, (((0,), (0,)), ((), ())), preferred_element_type=jnp.float32)


def pick_kernel(at, centers, weights, near, far, sems):
    first = pl.multiple_of(at[0] * 64, 64)
    half = pl.multiple_of(at[0] * 64 + at[1] * 32, 32)
    copies = [
        pltpu.make_async_copy(centers.at[pl.ds(first, 64), :], near.at[:, 0:1024], sems.at[0]),
        pltpu.make_async_copy(weights.at[pl.ds(first, 64), :], near.at[:, 1024:1280], sems.at[1]),
        pltpu.make_async_copy(centers.at[pl.ds(half, 32), :], far.at[:, 0:1024], sems.at[2]),
        pltpu.make_async_copy(weights.at[pl.ds(half, 32), :], far.at[:, 1024:1280], sems.at[3]),
    ]
    for copy in copies:
        copy.start()
    for copy in copies:
        copy.wait()


def pick(at, centers, weights):
    return pl.pallas_call(
        pick_kernel,
        in_specs=[SMEM] + [pl.BlockSpec(memory_space=pltpu.HBM)] * 2,
        out_specs=[VMEM] * 2,
        out_shape=[
            jax.ShapeDtypeStruct((64, 1280), jnp.float32),
            jax.ShapeDtypeStruct((32, 1280), jnp.float32),
        ],
        scratch_shapes=[pltpu.SemaphoreType.DMA((4,))],
        compiler_params=params(2),
        name="pick",
    )(at, *(pltpu.with_memory_space_constraint(v, pltpu.HBM) for v in (centers, weights)))


def rows_kernel(*refs):
    rows, (high, low, norm) = refs[:-3], refs[-3:]
    ones = jnp.ones((8, 1024), jnp.bfloat16)
    at = 0
    for ref in rows:
        value = ref[...]
        to = slice(at, at + value.shape[0])
        high[to, :], low[to, :] = halves(value)
        at += value.shape[0]
    for p in range(2):
        to = slice(p * 128, (p + 1) * 128)
        value = high[to, :].astype(jnp.float32) + low[to, :].astype(jnp.float32)
        square = value * value
        norm[:, to] = sum(dot_t(ones, v) for v in exact(square))


def convert_centers(refs, whole, outs):
    ch, cl, wh, wl, norm_c = outs
    at, refs = 0, list(refs)

    def convert(center, weight, at, count):
        to = pl.ds(at, count)
        square = center * center
        lanes = [square[:, i : i + 128] for i in range(0, 1024, 128)]
        norm_c[to, :] = sum(lanes[1:], lanes[0])
        ch[to, :], cl[to, :] = halves(center)
        wh[to, :], wl[to, :] = halves(weight)

    if whole:
        own_c, own_w = refs.pop(0), refs.pop(0)

        def step(i, carry):
            first = pl.multiple_of(i * 64, 64)
            to = pl.ds(first, 64)
            convert(own_c[to, :], own_w[to, :], first, 64)
            return carry

        lax.fori_loop(0, 4, step, 0)
        at = 256
    for ref in refs:
        count = ref.shape[0]
        convert(ref[:, 0:1024], ref[:, 1024:1280], at, count)
        at += count
    ones = jnp.ones((128, 128), jnp.bfloat16)
    norm_c[...] = sum(
        jnp.dot(v, ones, preferred_element_type=jnp.float32) for v in exact(norm_c[...])
    )


def tile_kernel(segments, has_before, *refs):
    refs = list(refs)
    take = lambda n: [refs.pop(0) for _ in range(n)]
    rh, rl, norm = take(3)
    inputs = [take(pieces or 5) for _, pieces, _ in segments]
    before = take(1) if has_before else None
    th, tl, pred = take(3)
    total = before[0][...] if has_before else None
    first = 0
    cross = refs.pop()
    for (count, pieces, whole), given in zip(segments, inputs):
        if pieces:
            centers = take(5)
            convert_centers(given, whole, centers)
        else:
            centers = given
        ch, cl, wh, wl, norm_c = centers
        cross[0:count, :] = three(dot_t, (ch[...], cl[...]), (rh[...], rl[...]))

        def step(i, carry):
            at = pl.multiple_of(i * 128, 128)
            here = pl.ds(at, 128)
            squared = norm[0:1, :] + norm_c[here, 0:1] - 2.0 * cross[here, :]
            to = pl.ds(pl.multiple_of(first + at, 128), 128)
            th[to, :], tl[to, :] = halves(jnp.exp(-jnp.sqrt(squared)))
            return carry

        lax.fori_loop(0, count // 128, step, 0)
        to = slice(first, first + count)
        part = three(dot_first, (wh[...], wl[...]), (th[to, :], tl[to, :]))
        total = part if total is None else total + part
        first += count
    if len(pred.shape) == 3:
        for p in range(2):
            pred[p] = total[:, p * 128 : (p + 1) * 128].T
    else:
        pred[...] = total


VMEM = pl.BlockSpec(memory_space=pltpu.VMEM)
SMEM = pl.BlockSpec(memory_space=pltpu.SMEM)


def params(mib):
    return pltpu.CompilerParams(vmem_limit_bytes=mib << 20)


def split_rows(rows):
    return pl.pallas_call(
        rows_kernel,
        in_specs=[VMEM] * len(rows),
        out_specs=[VMEM] * 3,
        out_shape=[
            jax.ShapeDtypeStruct((256, 1024), jnp.bfloat16),
            jax.ShapeDtypeStruct((256, 1024), jnp.bfloat16),
            jax.ShapeDtypeStruct((8, 256), jnp.float32),
        ],
        compiler_params=params(5),
    )(*rows)


def kernel_tile(side, segments, before, last):
    bf16, f32 = jnp.bfloat16, jnp.float32
    shape = jax.ShapeDtypeStruct
    args, spec, converted, count = list(side), [], [], 0
    for pieces, whole in segments:
        args += pieces
        raw = pieces[0].dtype == f32
        n = sum(p.shape[0] for p in pieces) - (256 if whole else 0) if raw else pieces[0].shape[0]
        spec.append((n, len(pieces) if raw else 0, whole))
        count += n
        if raw:
            converted += [shape((n, 1024), bf16)] * 2 + [shape((n, 256), bf16)] * 2
            converted.append(shape((n, 128), f32))
    args += [] if before is None else [before]
    outs = [shape((count, 256), bf16), shape((count, 256), bf16)]
    outs.append(shape((2, 128, 256) if last else (256, 256), f32))
    outs += converted
    out = pl.pallas_call(
        functools.partial(tile_kernel, spec, before is not None),
        in_specs=[VMEM] * len(args),
        out_specs=[VMEM] * len(outs),
        out_shape=outs,
        scratch_shapes=[pltpu.VMEM((max(n for n, _, _ in spec), 256), f32)],
        compiler_params=params(14),
    )(*args)
    return (out[0], out[1]), out[2], out[3:]


def assemble_kernel(at, *refs):
    tiles, (th, tl) = refs[:10], refs[10:]
    x, core = at[0], at[1]
    for low in range(2):
        full = (th, tl)[low]
        side_a, side_b = tiles[low:6:2], tiles[6 + low :: 2]

        def put(to, count, row):
            for cols, side in ((slice(0, 256), side_a), (slice(256, 512), side_b)):
                at = row
                for tile in side:
                    if 0 <= at < tile.shape[0]:
                        full[to, cols] = tile[at : at + count, :]
                    at -= tile.shape[0]

        put(slice(0, 256), 256, 0)
        for k in range(4):
            for swapped in range(2):
                piece = k * 2 + swapped
                half = lax.rem(core + swapped, 2)
                other = lax.rem(x + k, 4)
                to = pl.multiple_of((1 + 2 * half) * 256 + other * 64, 64)
                put(pl.ds(to, 64), 64, 256 + piece * 64)
                to = pl.multiple_of(512 + other * 64 + half * 32, 32)
                put(pl.ds(to, 32), 32, 768 + piece * 32)


def assemble(at, tiles):
    flat = [t for pair in tiles for t in pair]
    return pl.pallas_call(
        assemble_kernel,
        in_specs=[SMEM] + [VMEM] * len(flat),
        out_specs=[VMEM] * 2,
        out_shape=[jax.ShapeDtypeStruct((1024, 512), jnp.bfloat16)] * 2,
        compiler_params=params(8),
        name="assemble",
    )(at, *flat)


def gradient_kernel(offset, at, *refs):
    th, tl, resid, (out,) = refs[0], refs[1], refs[2:6], refs[6:7]
    rh, rl = refs[7:]
    half = pl.ds(pl.multiple_of(lax.rem(at[1] + offset, 2) * 128, 128), 128)
    for p in range(4):
        cols = slice(p * 128, (p + 1) * 128)
        rh[:, cols], rl[:, cols] = halves(resid[p][:, half].T)
    for m in range(4):
        cols = slice(m * 256, (m + 1) * 256)
        out[:, cols] = three(dot_t, (rh[...], rl[...]), (th[cols, :], tl[cols, :]))


def gradient(at, full, resid, offset):
    return pl.pallas_call(
        functools.partial(gradient_kernel, offset),
        in_specs=[SMEM] + [VMEM] * 6,
        out_specs=VMEM,
        out_shape=jax.ShapeDtypeStruct((128, 1024), jnp.float32),
        scratch_shapes=[pltpu.VMEM((128, 512), jnp.bfloat16)] * 2,
        compiler_params=params(8),
    )(at, *full, *resid)


BLOCK = ({}, {"yl": 1}, {"zl": 1}, {"zl": 1, "yl": 1})


def part(value, index, size, axis):
    return lax.dynamic_slice_in_dim(value, index * size, size, axis)


def named(value, **shift):
    return send(value, **shift)


REST = [list(range(core, 16, 2)) for core in range(2)]


def exchange(value):
    return lax.all_to_all(value, "batch", 0, 0, tiled=False, axis_index_groups=REST)


def to_z_neighbours(value):
    pairs = []
    for i in range(256):
        d = decode(i)
        d["zp"] += 1 if d["core"] else -1
        pairs.append((i, encode(d)))
    return lax.ppermute(value, AXES, pairs)


def step(batch_points, targets, centers, weights, eigen_basis, shrink):
    b = lax.axis_index("batch")
    x, core = b // 4, b % 2
    at = jnp.stack([x, core]).astype(jnp.int32)
    near, far = pick(at, centers, weights)
    near = to_z_neighbours(near)
    far = named(far, zp=2)
    rows_y = named(batch_points, yl=1)
    rows_z = named(batch_points, zl=1)
    near = [near] + [named(near, x=-k) for k in (1, 3, 2)]
    rows_d0 = named(rows_y[0:64], zl=1)
    far = [far] + [named(far, x=-k) for k in (1, 3, 2)]
    rows_d1 = named(rows_z[64:128], yl=1)
    near = [near[i] for i in (0, 1, 3, 2)]
    far = [far[i] for i in (0, 1, 3, 2)]
    near = [v for k in range(4) for v in (near[k], named(near[k], core=1))]
    far = [v for k in range(4) for v in (far[k], named(far[k], core=1))]
    side_a = split_rows((batch_points, rows_y))
    side_b = split_rows((rows_z, rows_d0, rows_d1))
    tile_a1, pred_a, first = kernel_tile(
        side_a, [([centers, weights, *near[:2]], True)], None, False
    )
    tile_a2, pred_a, second = kernel_tile(side_a, [(near[2:], False)], pred_a, False)
    tile_b1, pred_b, _ = kernel_tile(side_b, [(first, False), (second, False)], None, False)
    tile_b2, pred_b, third = kernel_tile(side_b, [(far, False)], pred_b, True)
    tile_a3, pred_a, _ = kernel_tile(side_a, [(third, False)], pred_a, True)
    pred = (pred_a[0], pred_a[1], pred_b[0], pred_b[1])
    residual = pred[0] - targets
    for p in (2, 3, 1):
        residual = residual + named(pred[p], **BLOCK[p])
    group = [residual] + [named(residual, **BLOCK[p]) for p in (1, 2, 3)]
    basis_near = to_z_neighbours(eigen_basis)
    basis_far = named(part(eigen_basis, core, 128, 0), zp=2)
    full = assemble(at, (tile_a1, tile_a2, tile_a3, tile_b1, tile_b2))
    give = gradient(at, full, group, 1)
    keep = gradient(at, full, group, 0)
    grad = keep + named(give, core=1)
    grad = exchange(grad.reshape(8, 16, 1024))
    grad = jnp.sum(grad, axis=0)
    places = (
        (eigen_basis, 0),
        (basis_near, 256 + 512 * core),
        (named(basis_near, core=1), 768 - 512 * core),
        (basis_far, 512 + 128 * core),
        (named(basis_far, core=1), 640 - 128 * core),
    )
    ordered = [lax.dynamic_slice_in_dim(grad, at, v.shape[0], 1) for v, at in places]
    basis = jnp.concatenate([v for v, _ in places])
    projected = jnp.dot(
        jnp.concatenate(ordered, axis=1),
        basis,
        precision=HI,
        preferred_element_type=jnp.float32,
    )
    both = {
        m: jnp.concatenate([grad[:, m * 256 : (m + 1) * 256], projected], axis=1)
        for m in range(4)
    }
    both = both[0] + sum(named(both[m], zp=m) for m in (2, 1, 3))
    both = both * (1.0 / math.sqrt(32768))
    grad, projected = both[:, 0:256], both[:, 256:768]
    projected = projected + sum(named(projected, **BLOCK[p]) for p in (3, 1, 2))
    correction = dot_t(projected * shrink[None, :], eigen_basis, HI)
    change = step_size * (grad - correction)
    change = exchange(jnp.broadcast_to(change[None], (8, 16, 256))).reshape(128, 256)
    other = named(change, core=1)
    both = jnp.where(core == 0, jnp.concatenate([change, other]), jnp.concatenate([other, change]))
    updated = weights - both.T
    return (residual, updated)


def solution(mesh):
    return jax.shard_map(
        step,
        mesh=mesh,
        in_specs=(
            P(("batch", "center"), None),
            P(("batch", "center"), None),
            P("center", None),
            P("center", None),
            P("center", None),
            P(),
        ),
        out_specs=(P(("batch", "center"), None), P("center", None)),
        check_vma=False,
    )
```

```python
import functools
import math

import jax
import jax.numpy as jnp
from jax import lax
from jax.experimental import pallas as pl
from jax.experimental.pallas import tpu as pltpu
from jax.sharding import PartitionSpec as P


step_size = 4.0
HI = lax.Precision.HIGHEST
AXES = ("center", "batch")


def decode(i):
    c, b = divmod(i, 16)
    return dict(zp=c // 4, zl=(c // 2) % 2, yl=c % 2, x=b // 4, yh=(b // 2) % 2, core=b % 2)


def encode(d):
    c = (d["zp"] % 4) * 4 + (d["zl"] % 2) * 2 + d["yl"] % 2
    return c * 16 + (d["x"] % 4) * 4 + (d["yh"] % 2) * 2 + d["core"] % 2


def send(value, **shift):
    pairs = []
    for i in range(256):
        d = decode(i)
        for name, by in shift.items():
            d[name] += by
        pairs.append((i, encode(d)))
    return lax.ppermute(value, AXES, pairs)


def dot_t(a, b, precision=None):
    return lax.dot_general(
        a, b, (((1,), (1,)), ((), ())), precision=precision, preferred_element_type=jnp.float32
    )


def halves(value):
    high = value.astype(jnp.bfloat16)
    return high, (value - high.astype(jnp.float32)).astype(jnp.bfloat16)


def exact(value):
    high, low = halves(value)
    rest = value - high.astype(jnp.float32) - low.astype(jnp.float32)
    return high, low, rest.astype(jnp.bfloat16)


def three(dot, a, b):
    return dot(a[0], b[0]) + dot(a[0], b[1]) + dot(a[1], b[0])


def dot_first(a, b):
    return lax.dot_general(a, b, (((0,), (0,)), ((), ())), preferred_element_type=jnp.float32)


def pick_kernel(at, centers, weights, near, far, sems):
    first = pl.multiple_of(at[0] * 64, 64)
    half = pl.multiple_of(at[0] * 64 + at[1] * 32, 32)
    copies = [
        pltpu.make_async_copy(centers.at[pl.ds(first, 64), :], near.at[:, 0:1024], sems.at[0]),
        pltpu.make_async_copy(weights.at[pl.ds(first, 64), :], near.at[:, 1024:1280], sems.at[1]),
        pltpu.make_async_copy(centers.at[pl.ds(half, 32), :], far.at[:, 0:1024], sems.at[2]),
        pltpu.make_async_copy(weights.at[pl.ds(half, 32), :], far.at[:, 1024:1280], sems.at[3]),
    ]
    for copy in copies:
        copy.start()
    for copy in copies:
        copy.wait()


def pick(at, centers, weights):
    return pl.pallas_call(
        pick_kernel,
        in_specs=[SMEM] + [pl.BlockSpec(memory_space=pltpu.HBM)] * 2,
        out_specs=[VMEM] * 2,
        out_shape=[
            jax.ShapeDtypeStruct((64, 1280), jnp.float32),
            jax.ShapeDtypeStruct((32, 1280), jnp.float32),
        ],
        scratch_shapes=[pltpu.SemaphoreType.DMA((4,))],
        compiler_params=params(2),
        name="pick",
    )(at, *(pltpu.with_memory_space_constraint(v, pltpu.HBM) for v in (centers, weights)))


def rows_kernel(*refs):
    rows, (high, low, norm) = refs[:-3], refs[-3:]
    ones = jnp.ones((8, 1024), jnp.bfloat16)
    at = 0
    for ref in rows:
        value = ref[...]
        to = slice(at, at + value.shape[0])
        high[to, :], low[to, :] = halves(value)
        at += value.shape[0]
    for p in range(2):
        to = slice(p * 128, (p + 1) * 128)
        value = high[to, :].astype(jnp.float32) + low[to, :].astype(jnp.float32)
        square = value * value
        norm[:, to] = sum(dot_t(ones, v) for v in exact(square))


def convert_centers(refs, whole, outs):
    ch, cl, wh, wl, norm_c = outs
    at, refs = 0, list(refs)

    def convert(center, weight, at, count):
        to = pl.ds(at, count)
        square = center * center
        lanes = [square[:, i : i + 128] for i in range(0, 1024, 128)]
        norm_c[to, :] = sum(lanes[1:], lanes[0])
        ch[to, :], cl[to, :] = halves(center)
        wh[to, :], wl[to, :] = halves(weight)

    if whole:
        own_c, own_w = refs.pop(0), refs.pop(0)

        def step(i, carry):
            first = pl.multiple_of(i * 64, 64)
            to = pl.ds(first, 64)
            convert(own_c[to, :], own_w[to, :], first, 64)
            return carry

        lax.fori_loop(0, 4, step, 0)
        at = 256
    for ref in refs:
        count = ref.shape[0]
        convert(ref[:, 0:1024], ref[:, 1024:1280], at, count)
        at += count
    ones = jnp.ones((128, 128), jnp.bfloat16)
    norm_c[...] = sum(
        jnp.dot(v, ones, preferred_element_type=jnp.float32) for v in exact(norm_c[...])
    )


def tile_kernel(segments, has_before, *refs):
    refs = list(refs)
    take = lambda n: [refs.pop(0) for _ in range(n)]
    rh, rl, norm = take(3)
    inputs = [take(pieces or 5) for _, pieces, _ in segments]
    before = take(1) if has_before else None
    th, tl, pred = take(3)
    total = before[0][...] if has_before else None
    first = 0
    cross = refs.pop()
    for (count, pieces, whole), given in zip(segments, inputs):
        if pieces:
            centers = take(5)
            convert_centers(given, whole, centers)
        else:
            centers = given
        ch, cl, wh, wl, norm_c = centers
        block = 192 if count % 192 == 0 else 128
        cross[0:count, :] = three(dot_t, (ch[...], cl[...]), (rh[...], rl[...]))

        def step(i, carry):
            at = pl.multiple_of(i * block, 64)
            here = pl.ds(at, block)
            squared = norm[0:1, :] + norm_c[here, 0:1] - 2.0 * cross[here, :]
            to = pl.ds(pl.multiple_of(first + at, 64), block)
            th[to, :], tl[to, :] = halves(jnp.exp(-jnp.sqrt(squared)))
            return carry

        lax.fori_loop(0, count // block, step, 0)
        to = slice(first, first + count)
        part = three(dot_first, (wh[...], wl[...]), (th[to, :], tl[to, :]))
        total = part if total is None else total + part
        first += count
    if len(pred.shape) == 3:
        for p in range(2):
            pred[p] = total[:, p * 128 : (p + 1) * 128].T
    else:
        pred[...] = total


VMEM = pl.BlockSpec(memory_space=pltpu.VMEM)
SMEM = pl.BlockSpec(memory_space=pltpu.SMEM)


def params(mib):
    return pltpu.CompilerParams(vmem_limit_bytes=mib << 20)


def split_rows(rows):
    return pl.pallas_call(
        rows_kernel,
        in_specs=[VMEM] * len(rows),
        out_specs=[VMEM] * 3,
        out_shape=[
            jax.ShapeDtypeStruct((256, 1024), jnp.bfloat16),
            jax.ShapeDtypeStruct((256, 1024), jnp.bfloat16),
            jax.ShapeDtypeStruct((8, 256), jnp.float32),
        ],
        compiler_params=params(5),
    )(*rows)


def kernel_tile(side, segments, before, last):
    bf16, f32 = jnp.bfloat16, jnp.float32
    shape = jax.ShapeDtypeStruct
    args, spec, converted, count = list(side), [], [], 0
    for pieces, whole in segments:
        args += pieces
        raw = pieces[0].dtype == f32
        n = sum(p.shape[0] for p in pieces) - (256 if whole else 0) if raw else pieces[0].shape[0]
        spec.append((n, len(pieces) if raw else 0, whole))
        count += n
        if raw:
            converted += [shape((n, 1024), bf16)] * 2 + [shape((n, 256), bf16)] * 2
            converted.append(shape((n, 128), f32))
    args += [] if before is None else [before]
    outs = [shape((count, 256), bf16), shape((count, 256), bf16)]
    outs.append(shape((2, 128, 256) if last else (256, 256), f32))
    outs += converted
    out = pl.pallas_call(
        functools.partial(tile_kernel, spec, before is not None),
        in_specs=[VMEM] * len(args),
        out_specs=[VMEM] * len(outs),
        out_shape=outs,
        scratch_shapes=[pltpu.VMEM((max(n for n, _, _ in spec), 256), f32)],
        compiler_params=params(14),
    )(*args)
    return (out[0], out[1]), out[2], out[3:]


def assemble_kernel(at, *refs):
    tiles, (th, tl) = refs[:10], refs[10:]
    x, core = at[0], at[1]
    for low in range(2):
        full = (th, tl)[low]
        side_a, side_b = tiles[low:6:2], tiles[6 + low :: 2]

        def put(to, count, row):
            for cols, side in ((slice(0, 256), side_a), (slice(256, 512), side_b)):
                at = row
                for tile in side:
                    if 0 <= at < tile.shape[0]:
                        full[to, cols] = tile[at : at + count, :]
                    at -= tile.shape[0]

        put(slice(0, 256), 256, 0)
        for k in range(4):
            for swapped in range(2):
                piece = k * 2 + swapped
                half = lax.rem(core + swapped, 2)
                other = lax.rem(x + k, 4)
                to = pl.multiple_of((1 + 2 * half) * 256 + other * 64, 64)
                put(pl.ds(to, 64), 64, 256 + piece * 64)
                to = pl.multiple_of(512 + other * 64 + half * 32, 32)
                put(pl.ds(to, 32), 32, 768 + piece * 32)


def assemble(at, tiles):
    flat = [t for pair in tiles for t in pair]
    return pl.pallas_call(
        assemble_kernel,
        in_specs=[SMEM] + [VMEM] * len(flat),
        out_specs=[VMEM] * 2,
        out_shape=[jax.ShapeDtypeStruct((1024, 512), jnp.bfloat16)] * 2,
        compiler_params=params(8),
        name="assemble",
    )(at, *flat)


def gradient_kernel(offset, at, *refs):
    th, tl, resid, (out,) = refs[0], refs[1], refs[2:6], refs[6:7]
    rh, rl = refs[7:]
    half = pl.ds(pl.multiple_of(lax.rem(at[1] + offset, 2) * 128, 128), 128)
    for p in range(4):
        cols = slice(p * 128, (p + 1) * 128)
        rh[:, cols], rl[:, cols] = halves(resid[p][:, half].T)
    for m in range(4):
        cols = slice(m * 256, (m + 1) * 256)
        out[:, cols] = three(dot_t, (rh[...], rl[...]), (th[cols, :], tl[cols, :]))


def gradient(at, full, resid, offset):
    return pl.pallas_call(
        functools.partial(gradient_kernel, offset),
        in_specs=[SMEM] + [VMEM] * 6,
        out_specs=VMEM,
        out_shape=jax.ShapeDtypeStruct((128, 1024), jnp.float32),
        scratch_shapes=[pltpu.VMEM((128, 512), jnp.bfloat16)] * 2,
        compiler_params=params(8),
    )(at, *full, *resid)


BLOCK = ({}, {"yl": 1}, {"zl": 1}, {"zl": 1, "yl": 1})


def part(value, index, size, axis):
    return lax.dynamic_slice_in_dim(value, index * size, size, axis)


def named(value, **shift):
    return send(value, **shift)


REST = [list(range(core, 16, 2)) for core in range(2)]


def exchange(value):
    return lax.all_to_all(value, "batch", 0, 0, tiled=False, axis_index_groups=REST)


def to_z_neighbours(value):
    pairs = []
    for i in range(256):
        d = decode(i)
        d["zp"] += 1 if d["core"] else -1
        pairs.append((i, encode(d)))
    return lax.ppermute(value, AXES, pairs)


def step(batch_points, targets, centers, weights, eigen_basis, shrink):
    b = lax.axis_index("batch")
    x, core = b // 4, b % 2
    at = jnp.stack([x, core]).astype(jnp.int32)
    near, far = pick(at, centers, weights)
    near = to_z_neighbours(near)
    far = named(far, zp=2)
    rows_y = named(batch_points, yl=1)
    rows_z = named(batch_points, zl=1)
    near = [near] + [named(near, x=-k) for k in (1, 3, 2)]
    rows_d0 = named(rows_y[0:64], zl=1)
    far = [far] + [named(far, x=-k) for k in (1, 3, 2)]
    rows_d1 = named(rows_z[64:128], yl=1)
    near = [near[i] for i in (0, 1, 3, 2)]
    far = [far[i] for i in (0, 1, 3, 2)]
    near = [v for k in range(4) for v in (near[k], named(near[k], core=1))]
    far = [v for k in range(4) for v in (far[k], named(far[k], core=1))]
    side_a = split_rows((batch_points, rows_y))
    side_b = split_rows((rows_z, rows_d0, rows_d1))
    tile_a1, pred_a, first = kernel_tile(
        side_a, [([centers, weights, *near[:2]], True)], None, False
    )
    tile_a2, pred_a, second = kernel_tile(side_a, [(near[2:], False)], pred_a, False)
    tile_b1, pred_b, _ = kernel_tile(side_b, [(first, False), (second, False)], None, False)
    tile_b2, pred_b, third = kernel_tile(side_b, [(far, False)], pred_b, True)
    tile_a3, pred_a, _ = kernel_tile(side_a, [(third, False)], pred_a, True)
    pred = (pred_a[0], pred_a[1], pred_b[0], pred_b[1])
    residual = pred[0] - targets
    for p in (2, 3, 1):
        residual = residual + named(pred[p], **BLOCK[p])
    group = [residual] + [named(residual, **BLOCK[p]) for p in (1, 2, 3)]
    basis_near = to_z_neighbours(eigen_basis)
    basis_far = named(part(eigen_basis, core, 128, 0), zp=2)
    full = assemble(at, (tile_a1, tile_a2, tile_a3, tile_b1, tile_b2))
    give = gradient(at, full, group, 1)
    keep = gradient(at, full, group, 0)
    grad = keep + named(give, core=1)
    grad = exchange(grad.reshape(8, 16, 1024))
    grad = jnp.sum(grad, axis=0)
    places = (
        (eigen_basis, 0),
        (basis_near, 256 + 512 * core),
        (named(basis_near, core=1), 768 - 512 * core),
        (basis_far, 512 + 128 * core),
        (named(basis_far, core=1), 640 - 128 * core),
    )
    ordered = [lax.dynamic_slice_in_dim(grad, at, v.shape[0], 1) for v, at in places]
    basis = jnp.concatenate([v for v, _ in places])
    projected = jnp.dot(
        jnp.concatenate(ordered, axis=1),
        basis,
        precision=HI,
        preferred_element_type=jnp.float32,
    )
    both = {
        m: jnp.concatenate([grad[:, m * 256 : (m + 1) * 256], projected], axis=1)
        for m in range(4)
    }
    both = both[0] + sum(named(both[m], zp=m) for m in (2, 1, 3))
    both = both * (1.0 / math.sqrt(32768))
    grad, projected = both[:, 0:256], both[:, 256:768]
    projected = projected + sum(named(projected, **BLOCK[p]) for p in (3, 1, 2))
    correction = dot_t(projected * shrink[None, :], eigen_basis, HI)
    change = step_size * (grad - correction)
    change = exchange(jnp.broadcast_to(change[None], (8, 16, 256))).reshape(128, 256)
    other = named(change, core=1)
    both = jnp.where(core == 0, jnp.concatenate([change, other]), jnp.concatenate([other, change]))
    updated = weights - both.T
    return (residual, updated)


def solution(mesh):
    return jax.shard_map(
        step,
        mesh=mesh,
        in_specs=(
            P(("batch", "center"), None),
            P(("batch", "center"), None),
            P("center", None),
            P("center", None),
            P("center", None),
            P(),
        ),
        out_specs=(P(("batch", "center"), None), P("center", None)),
        check_vma=False,
    )
```
